32 devices in a mesh: groups: 2 (over y), tmpl: 4 (over z), region: 2 (over x), sub: 2 (over core).
Axes of the slice: x: 2, y: 2, z: 4, core: 2. Of those that a mesh axis runs over, the one named last changes fastest.
Arguments:
- waveforms: float32 [2, 16, 4096], P('region', ('tmpl', 'sub'), 'groups'), parts along dimension 2
- templates: bfloat16 [2, 192, 12, 400], P('region', ('tmpl', 'sub'))
- channel_ids: int32 [2, 192, 12], P('region', ('tmpl', 'sub')), may hold values from 0 to 31, as said below
- moveouts: int32 [2, 192, 12], P('region', ('tmpl', 'sub')), may hold values from 0 to 511
- active: int32 [2, 192], P('region', ('tmpl', 'sub')), may hold values from 6 to 12
- border: int32 [2, 2, 8], P('region'), may hold values from 0 to 15, as said below
- border_count: int32 [2, 2], P('region'), may hold values from 1 to 8
Outputs:
- scores: float32 [2, 192, 1024], P('region', ('tmpl', 'sub'), 'groups'), parts along dimension 2
The draws below stay inside these ranges and needn't reach their ends.
There are 2 independent parts, one for each index of `groups`. The reference program is written for one: setup_inputs(seed, part) draws one part's arguments, and reference() takes and returns one part's arrays. A program takes and returns all parts, laid end to end along the dimension named above; an argument that names none is the same for every part. Nothing has to cross between parts.
Inputs may be any that keep to these rules, and one draw needn't show every extreme that they name: `channel_ids`: the 12 entries of a template are distinct. An entry below 16 is one of the region's own channels; 16 + i is entry i of the previous region's side 1 border list and 24 + i entry i of the next region's side 0 border list; such an entry appears only where that region exists and i is below that list's border_count. `border`: each list names 8 distinct channels of its region.
All inputs are finite; a program needn't handle non-finite values.
Results may differ from the reference program's by a relative error of at most 0.0081.
Values sent between devices are 32-bit elements; how exact they have to be, the bound alone decides.
A program may use at most 64 MiB of HBM per device.

```python
import math
import jax
import jax.numpy as jnp
from jax import lax

NF = 2048
F0 = 40
BAND = 384
K = 400
SLOTS = 12
MINACT = 6
OUT = 512
SHMAX = 512
LN = 1024
REGIONS = 2
CH_REG = 16
BMAX = 8
CH_EXT = 32
TPL_REG = 192


def draw_waveforms(key, part):
    keys = jax.random.split(jax.random.fold_in(key, 11), 9)
    amplitude = jnp.exp(jax.random.uniform(keys[0], (REGIONS, CH_REG, 1), jnp.float32, 0.0, math.log(10.0)))
    centers = jax.random.uniform(keys[1], (REGIONS, CH_REG, 3, 1), jnp.float32, 0.0, NF * 1.0)
    heights = jnp.exp(jax.random.uniform(keys[2], (REGIONS, CH_REG, 3, 1), jnp.float32, 0.0, math.log(8.0)))
    samples = jnp.arange(NF, dtype=jnp.float32)[None, None, None, :]
    spread = NF / 16.0
    envelope = 1.0 + jnp.sum(heights * jnp.exp(-0.5 * jnp.square((samples - centers) / spread)), axis=2)
    noise = jax.random.normal(keys[3], (REGIONS, CH_REG, NF), jnp.float32)
    spike_on = (jax.random.randint(keys[5], (REGIONS, CH_REG, 1), 0, 100, jnp.int32) < 12).astype(jnp.float32)
    positions = jax.random.randint(keys[6], (REGIONS, CH_REG, 3, 1), 0, NF, jnp.int32)
    signs = (2 * jax.random.randint(keys[7], (REGIONS, CH_REG, 3, 1), 0, 2, jnp.int32) - 1).astype(jnp.float32)
    spike_sizes = signs * jax.random.uniform(keys[8], (REGIONS, CH_REG, 3, 1), jnp.float32, 40.0, 100.0)
    sample_ids = jnp.arange(NF, dtype=jnp.int32)[None, None, None, :]
    spikes = jnp.sum(jnp.where(sample_ids == positions, spike_sizes, 0.0), axis=2) * spike_on
    return (amplitude * (envelope * noise + spikes)).astype(jnp.float32)


def draw_templates(key, part):
    keys = jax.random.split(jax.random.fold_in(key, 22), 2)
    scaling = jnp.exp(jax.random.uniform(keys[0], (REGIONS, TPL_REG, SLOTS, 1), jnp.float32, 0.0, math.log(10.0)))
    shapes = jax.random.normal(keys[1], (REGIONS, TPL_REG, SLOTS, K), jnp.float32)
    return (scaling * shapes).astype(jnp.bfloat16)


def border_sizes(key):
    keys = jax.random.split(jax.random.fold_in(key, 33), 2)
    sizes = jax.random.randint(keys[0], (REGIONS, 2), 1, BMAX + 1, jnp.int32)
    forced = jax.random.randint(keys[1], (), 1, REGIONS, jnp.int32)
    sizes = sizes.at[forced, 0].set(BMAX)
    sizes = sizes.at[0, 0].set(1)
    return (sizes, forced)


def draw_border_count(key, part):
    return border_sizes(key)[0]


def draw_border(key, part):
    slot_ids = jnp.arange(CH_REG, dtype=jnp.int32)
    scores = jax.random.randint(jax.random.fold_in(key, 44), (REGIONS, 2, CH_REG), 0, 1 << 20, jnp.int32) * CH_REG + slot_ids
    scores = scores.at[0, 0, 0].set(1 << 30)
    scores = scores.at[0, 0, CH_REG - 1].set((1 << 30) + 1)
    return lax.top_k(scores, BMAX)[1].astype(jnp.int32)


def draw_channel_ids(key, part):
    sizes, forced = border_sizes(key)
    keys = jax.random.split(jax.random.fold_in(key, 55), 2)
    slot_ids = jnp.arange(CH_EXT, dtype=jnp.int32)[None, :]
    region_ids = jnp.arange(REGIONS, dtype=jnp.int32)[:, None]
    left_live = jnp.where(region_ids > 0, sizes[jnp.maximum(region_ids - 1, 0), 1], 0)
    right_live = jnp.where(region_ids < REGIONS - 1, sizes[jnp.minimum(region_ids + 1, REGIONS - 1), 0], 0)
    left_slot = slot_ids - CH_REG
    right_slot = slot_ids - CH_REG - BMAX
    valid = (slot_ids < CH_REG) | (left_slot >= 0) & (left_slot < BMAX) & (left_slot < left_live) | (right_slot >= 0) & (right_slot < right_live)
    scores = jax.random.randint(keys[0], (REGIONS, TPL_REG, CH_EXT), 0, 1 << 20, jnp.int32) * CH_EXT + slot_ids[None]
    scores = jnp.where(valid[:, None, :], scores, -1)
    picked = jax.random.randint(keys[1], (), 0, TPL_REG, jnp.int32)
    template_ids = jnp.arange(TPL_REG, dtype=jnp.int32)[None, :, None]
    boost = (region_ids[:, :, None] == forced - 1) & (template_ids == picked) & ((slot_ids[None] == 0) | (slot_ids[None] == CH_EXT - 1))
    scores = jnp.where(boost, (1 << 30) + slot_ids[None], scores)
    return lax.top_k(scores, SLOTS)[1].astype(jnp.int32)


def touch_ends(result, own_key, smallest, top_value):
    longest = result.shape.index(max(result.shape))
    spots = []
    for shift in (0, 1):
        where = [jax.random.randint(jax.random.fold_in(own_key, axis), (), 0, length) for axis, length in enumerate(result.shape)]
        where[longest] = (where[longest] + shift) % result.shape[longest]
        spots.append(tuple(where))
    return result.at[spots[0]].set(smallest).at[spots[1]].set(top_value)


def setup_inputs(seed: int = 0, part: int = 0) -> dict:
    seeds = jax.random.split(jax.random.key(seed), 8)
    part_splits = jax.random.split(jax.random.fold_in(seeds[7], part), 8)
    return {
        "waveforms": draw_waveforms(jax.random.fold_in(jax.random.fold_in(seeds[7], part), 71), part),
        "templates": draw_templates(jax.random.fold_in(seeds[7], 71), part),
        "channel_ids": draw_channel_ids(jax.random.fold_in(seeds[7], 71), part),
        "moveouts": touch_ends(jax.random.randint(seeds[3], (REGIONS, TPL_REG, SLOTS), 0, SHMAX), jax.random.fold_in(seeds[3], 1), 0, SHMAX - 1).astype(jnp.int32),
        "active": touch_ends(jax.random.randint(seeds[4], (REGIONS, TPL_REG), MINACT, SLOTS + 1), jax.random.fold_in(seeds[4], 1), MINACT, SLOTS).astype(jnp.int32),
        "border": draw_border(jax.random.fold_in(seeds[7], 71), part),
        "border_count": draw_border_count(jax.random.fold_in(seeds[7], 71), part),
    }


EPSILON = 1e-06

def angles(samples, first_bin, bins, length):
    sample_ids = jnp.arange(samples, dtype=jnp.int32)[:, None]
    bin_ids = first_bin + jnp.arange(bins, dtype=jnp.int32)[None, :]
    turn_count = sample_ids * bin_ids % length
    return turn_count.astype(jnp.float32) * (2.0 * math.pi / length)

def forward_table(samples, first_bin, bins, length):
    phases = angles(samples, first_bin, bins, length)
    return jnp.concatenate([jnp.cos(phases), -jnp.sin(phases)], axis=1)

def inverse_table(samples, first_bin, bins, length):
    phases = jnp.transpose(angles(samples, first_bin, bins, length))
    return jnp.concatenate([jnp.cos(phases), -jnp.sin(phases)], axis=0)

def window_energy(spectra):
    lag_rows = inverse_table(NF, F0, BAND, NF)
    filtered = 2.0 / NF * jnp.dot(spectra, lag_rows, precision=lax.Precision.HIGHEST, preferred_element_type=jnp.float32)
    running = jnp.cumsum(filtered * filtered, axis=1)
    running = jnp.concatenate([jnp.zeros((running.shape[0], 1), jnp.float32), running], axis=1)
    return running[:, K:K + LN] - running[:, :LN]

def pick_rows(payload, indices, live_count, offset):
    chosen = jnp.take(payload, indices, axis=0)
    places = offset + jnp.arange(indices.shape[0], dtype=jnp.int32)
    return jnp.where((places < live_count)[:, None], chosen, jnp.zeros_like(chosen))

def cross_spectrum(tmpl_spectra, data_spectra):
    half_bins = tmpl_spectra.shape[1] // 2
    tmpl_real = tmpl_spectra[:, :half_bins]
    tmpl_imag = tmpl_spectra[:, half_bins:]
    data_real = data_spectra[:, :half_bins]
    data_imag = data_spectra[:, half_bins:]
    return jnp.concatenate([tmpl_real * data_real + tmpl_imag * data_imag, tmpl_real * data_imag - tmpl_imag * data_real], axis=1)

def block_scores(block_items, ext_spectra, station_norm, short_table, lag_table):
    block_waves, block_ids, block_moves, block_active = block_items
    templ_count = block_waves.shape[0]
    slot_count = block_waves.shape[1]
    flat_waves = block_waves.reshape(templ_count * slot_count, block_waves.shape[2]).astype(jnp.float32)
    tmpl_spectra = jnp.dot(flat_waves, short_table, precision=lax.Precision.HIGHEST, preferred_element_type=jnp.float32)
    tmpl_norm = jnp.sqrt(lax.optimization_barrier(jnp.sum(jnp.square(flat_waves), axis=1)) + EPSILON)
    flat_ids = block_ids.reshape(-1)
    cross_terms = cross_spectrum(tmpl_spectra, jnp.take(ext_spectra, flat_ids, axis=0)).astype(jnp.bfloat16)
    cross_terms = lax.optimization_barrier(cross_terms).astype(jnp.float32)
    correlation = 2.0 / NF * jnp.dot(cross_terms, lag_table, precision=lax.Precision.HIGHEST, preferred_element_type=jnp.float32)
    normed = correlation / (tmpl_norm[:, None] * jnp.take(station_norm, flat_ids, axis=0))
    aligned = jax.vmap(lambda series, offset: lax.dynamic_slice_in_dim(series, offset, OUT))(normed, block_moves.reshape(-1).astype(jnp.int32))
    weights = (jnp.arange(slot_count, dtype=jnp.int32)[None, :] < block_active[:, None]).astype(jnp.float32)
    return lax.optimization_barrier(jnp.sum(aligned.reshape(templ_count, slot_count, OUT) * weights[:, :, None], axis=1))

def reference(waveforms, templates, channel_ids, moveouts, active, border, border_count):
    data_table = forward_table(NF, F0, BAND, NF)
    spectra = lax.map(lambda trace: jnp.dot(trace, data_table, precision=lax.Precision.HIGHEST, preferred_element_type=jnp.float32), waveforms)
    energy = lax.map(window_energy, spectra)
    payload = jnp.concatenate([spectra, energy], axis=2)
    right_rows = jax.vmap(pick_rows, in_axes=(0, 0, 0, None))(payload, border[:, 1], border_count[:, 1], 0)
    left_rows = jax.vmap(pick_rows, in_axes=(0, 0, 0, None))(payload, border[:, 0], border_count[:, 0], 0)
    blank = jnp.zeros_like(right_rows[:1])
    from_left = jnp.concatenate([blank, right_rows[:-1]], axis=0)
    from_right = jnp.concatenate([left_rows[1:], blank], axis=0)
    extended = jnp.concatenate([payload, from_left, from_right], axis=1)
    short_table = lax.optimization_barrier(forward_table(K, F0, BAND, NF).astype(jnp.bfloat16)).astype(jnp.float32)
    lag_table = lax.optimization_barrier(inverse_table(LN, F0, BAND, NF).astype(jnp.bfloat16)).astype(jnp.float32)

    def region_scores(region_items):
        ext_rows, region_waves, region_ids, region_moves, region_active = region_items
        ext_spectra = ext_rows[:, :2 * BAND]
        station_norm = jnp.sqrt(ext_rows[:, 2 * BAND:] + EPSILON)
        templ_total = region_waves.shape[0]
        block_size = 48 if templ_total % 48 == 0 else templ_total
        block_total = templ_total // block_size

        def run_block(block_items):
            return block_scores(block_items, ext_spectra, station_norm, short_table, lag_table)
        stacked = lax.map(run_block, (region_waves.reshape(block_total, block_size, SLOTS, K), region_ids.reshape(block_total, block_size, SLOTS), region_moves.reshape(block_total, block_size, SLOTS), region_active.reshape(block_total, block_size)))
        return stacked.reshape(templ_total, OUT)
    return lax.map(region_scores, (extended, templates, channel_ids, moveouts, active))
```

```python
import functools

import jax
import jax.numpy as jnp
import ml_dtypes
import numpy as np
from jax import lax
from jax.experimental import pallas as pl
from jax.experimental.pallas import tpu as pltpu
from jax.sharding import PartitionSpec as P

NF = 2048
F0 = 40
BAND = 384
K = 400
OUT = 512
LN = 1024
EPSILON = 1e-06

LANES = 128
RES = NF // LANES
STEPS = BAND // RES
CHUNKS = (2 * BAND + LN) // LANES
SPEC_CHUNKS = 2 * BAND // LANES
MESH = pl.DeviceIdType.MESH
HIGH = lax.Precision.HIGHEST


def dot(a, b):
    return jnp.dot(a, b, precision=HIGH, preferred_element_type=jnp.float32)


def bin_order():
    r, g = np.meshgrid(np.arange(RES), np.arange(STEPS), indexing="ij")
    return (F0 + RES * g + r).reshape(-1)


def wide_tables():
    bins = bin_order()
    turn = 2.0 * np.pi / NF
    short = (np.arange(K)[:, None] * bins[None, :] % NF) * turn
    short = np.concatenate([np.cos(short), -np.sin(short)], axis=1)
    lag = (bins[:, None] * np.arange(LN)[None, :] % NF) * turn
    lag = np.concatenate([np.cos(lag), -np.sin(lag)], axis=0)
    as_bf16 = lambda x: x.astype(np.float32).astype(ml_dtypes.bfloat16)
    return as_bf16(short), as_bf16(lag)


def small_tables(chans):
    turn = 2.0 * np.pi / NF
    r, a, b, g = np.arange(RES), np.arange(RES), np.arange(LANES), np.arange(STEPS)
    eye = np.eye(chans)
    alpha = (F0 + r)[:, None] * a[None, :] * LANES % NF * turn
    gather = np.concatenate([np.kron(np.cos(alpha), eye), np.kron(-np.sin(alpha), eye)], axis=0)
    spread = 2.0 / NF * np.concatenate(
        [np.kron(np.cos(alpha.T), eye), np.kron(-np.sin(alpha.T), eye)], axis=1
    )
    theta = np.repeat((F0 + r)[:, None] * b[None, :] % NF * turn, chans, axis=0)
    twiddle = np.concatenate([np.cos(theta), np.sin(theta)], axis=0)
    beta = b[:, None] * g[None, :] * RES % NF * turn
    c, s = np.cos(beta), np.sin(beta)
    fwd = np.zeros((2 * LANES, LANES))
    fwd[:LANES, :STEPS], fwd[:LANES, STEPS : 2 * STEPS] = c, -s
    fwd[LANES:, :STEPS], fwd[LANES:, STEPS : 2 * STEPS] = s, c
    inv = np.zeros((LANES, 2 * LANES))
    inv[:STEPS, :LANES], inv[:STEPS, LANES:] = c.T, s.T
    inv[STEPS : 2 * STEPS, :LANES], inv[STEPS : 2 * STEPS, LANES:] = -s.T, c.T
    rows = []
    for i in (0, 1, 3, 4):
        place = LANES * i + b[:, None] - b[None, :]
        rows.append((place >= 0) & (place < K))
    window = np.concatenate(rows, axis=0)
    return [x.astype(np.float32) for x in (gather, spread, twiddle, fwd, inv, window)]


def station_kernel(
    geometry, wave_ref, border_ref, count_ref, tmpl_ref, short_ref, gather_ref, spread_ref,
    twiddle_ref, fwd_ref, inv_ref, window_ref, recv_ref, tspec_ref, scale_ref,
    pay_ref, rows_ref, spec_ref, pad_ref, send_sem, recv_sem,
):
    regions, tmpls, subs, offsets = geometry
    group = tmpls * subs
    region = lax.axis_index("region")
    place = lax.axis_index("tmpl") * subs + lax.axis_index("sub")
    peers = []
    for block, offset in enumerate(offsets):
        there = lax.rem(region + (regions - offset) % regions, regions)
        for step in range(1 if offset == 0 else 0, group):
            peer = lax.rem(place + step, group)
            device = {"region": there, "tmpl": peer // subs, "sub": lax.rem(peer, subs)}
            peers.append((block, step, peer, device))
    barrier = pltpu.get_barrier_semaphore()
    for _, _, _, device in peers:
        pl.semaphore_signal(barrier, inc=1, device_id=device, device_id_type=MESH)

    chans = wave_ref.shape[0]
    half = RES * chans
    for a in range(RES):
        rows_ref[chans * a : chans * (a + 1), :] = wave_ref[:, LANES * a : LANES * (a + 1)]
    y = dot(gather_ref[...], rows_ref[...])
    cos, sin = twiddle_ref[:half, :], twiddle_ref[half:, :]
    yr, yi = y[:half], y[half:]
    z = jnp.concatenate([yr * cos + yi * sin, yi * cos - yr * sin], axis=1)
    x = dot(z, fwd_ref[...])
    for r in range(RES):
        piece = x[chans * r : chans * (r + 1), :]
        spec_ref[:, STEPS * r : STEPS * (r + 1)] = piece[:, :STEPS]
        spec_ref[:, BAND + STEPS * r : BAND + STEPS * (r + 1)] = piece[:, STEPS : 2 * STEPS]
    for k in range(SPEC_CHUNKS):
        pay_ref[chans * k : chans * (k + 1), :] = spec_ref[:, LANES * k : LANES * (k + 1)]
    v = dot(x, inv_ref[...])
    vr, vi = v[:, :LANES], v[:, LANES:]
    u = jnp.concatenate([vr * cos - vi * sin, vr * sin + vi * cos], axis=0)
    filtered = dot(spread_ref[...], u)
    rows_ref[...] = filtered * filtered
    count = LN // LANES * chans
    near = lambda i: rows_ref[chans * i : chans * i + count, :]
    pieces = jnp.concatenate([near(0), near(1) + near(2), near(3), near(4)], axis=1)
    start = chans * SPEC_CHUNKS
    pay_ref[start : start + count, :] = dot(pieces, window_ref[...])
    bmax = border_ref.shape[1]
    base = chans * CHUNKS
    pay_ref[base:, :] = jnp.zeros((pay_ref.shape[0] - base, LANES), jnp.float32)
    pay_ref[base : base + 1, :bmax] = border_ref[1:2, :].astype(jnp.float32)
    pay_ref[base + 1 : base + 2, :bmax] = border_ref[0:1, :].astype(jnp.float32)
    pay_ref[base + 2 : base + 3, :2] = count_ref[...].astype(jnp.float32)

    pl.semaphore_wait(barrier, len(peers))
    copies = []
    for block, step, peer, device in peers:
        copy = pltpu.make_async_remote_copy(
            src_ref=pay_ref,
            dst_ref=recv_ref.at[block * group + place],
            send_sem=send_sem.at[block * group + step],
            recv_sem=recv_sem.at[block * group + place],
            device_id=device,
            device_id_type=MESH,
        )
        copy.start()
        copies.append(copy)
    recv_ref[pl.ds(place, 1)] = pay_ref[...][None]

    templs, slots, _ = tmpl_ref.shape
    pad_ref[...] = jnp.zeros_like(pad_ref)
    for t in range(templs):
        pad_ref[t, :slots, :] = tmpl_ref[t]
    waves = pad_ref[...].reshape(templs * pad_ref.shape[1], K)
    tspec_ref[...] = jnp.dot(waves, short_ref[...], preferred_element_type=jnp.float32)
    wide = waves.astype(jnp.float32)
    power = jnp.sum(wide * wide, axis=1, keepdims=True)
    scale_ref[...] = 2.0 / NF * lax.rsqrt(power + EPSILON)

    for copy in copies:
        copy.wait_send()
    for block, step, peer, device in peers:
        slot = block * group + peer
        pltpu.make_async_remote_copy(
            src_ref=pay_ref,
            dst_ref=recv_ref.at[slot],
            send_sem=send_sem.at[block * group + step],
            recv_sem=recv_sem.at[slot],
            device_id=device,
            device_id_type=MESH,
        ).wait_recv()


def match_kernel(
    geometry, chans, bmax, recv_ref, tspec_ref, scale_ref, ids_ref, move_ref, active_ref, lag_ref,
    out_ref, table_ref, parts_ref, cross_ref, line_ref, sums_ref,
):
    regions, tmpls, subs, offsets = geometry
    group = tmpls * subs
    own = group * chans
    total = own * len(offsets)
    ext = own + 2 * bmax
    templs, slots = ids_ref.shape
    padded = tspec_ref.shape[0] // templs
    wide = padded * templs
    bf16, f32 = jnp.bfloat16, jnp.float32

    for d in range(group * len(offsets)):
        for k in range(CHUNKS):
            table_ref[chans * d : chans * (d + 1), LANES * k : LANES * (k + 1)] = recv_ref[
                d, chans * k : chans * (k + 1), :
            ]
    table_ref[:, 2 * BAND :] = lax.rsqrt(table_ref[:, 2 * BAND :] + EPSILON)
    table = table_ref[...]
    high = table.astype(bf16)
    rest = table - high.astype(f32)
    middle = rest.astype(bf16)
    low = (rest - middle.astype(f32)).astype(bf16)
    parts_ref[...] = jnp.concatenate([high, middle, low], axis=0)

    region = lax.axis_index("region")
    left = offsets.index((regions - 1) % regions)
    right = offsets.index(1 % regions)
    base = chans * CHUNKS
    lane = lax.broadcasted_iota(jnp.int32, (1, LANES), 1)
    info = recv_ref[left * group, base : base + 3, :]
    from_left = info[0:1].astype(jnp.int32)
    left_count = jnp.where(region > 0, info[2:3, 1:2].astype(jnp.int32), 0)
    info = recv_ref[right * group, base : base + 3, :]
    from_right = info[1:2].astype(jnp.int32)
    right_count = jnp.where(region < regions - 1, info[2:3, 0:1].astype(jnp.int32), 0)
    row = lax.broadcasted_iota(jnp.int32, (3 * total, 1), 0) % total
    one = lambda mask: jnp.where(mask, 1.0, 0.0).astype(bf16)
    own_pick = one(row == lane[:, :own])
    left_pick = one((row == left * own + from_left[:, :bmax]) & (lane[:, :bmax] < left_count))
    right_pick = one((row == right * own + from_right[:, :bmax]) & (lane[:, :bmax] < right_count))

    slot_row = lax.broadcasted_iota(jnp.int32, (wide, 1), 0)
    spread = one(slot_row // padded == lax.broadcasted_iota(jnp.int32, (wide, templs), 1))
    ids = ids_ref[...].astype(f32).astype(bf16)
    ids = jnp.dot(spread, ids, preferred_element_type=f32)
    mine = slot_row % padded == lax.broadcasted_iota(jnp.int32, (wide, slots), 1)
    ids = jnp.sum(jnp.where(mine, ids, 0.0), axis=1, keepdims=True).astype(jnp.int32)
    contract = (((1,), (1,)), ((), ()))
    pick = lambda first, rows_pick: lax.dot_general(
        one(ids == first + lane[:, : rows_pick.shape[1]]), rows_pick, contract,
        preferred_element_type=f32,
    )
    chosen = pick(0, own_pick) + pick(own, left_pick) + pick(own + bmax, right_pick)
    chosen = chosen.astype(bf16)

    spec = jnp.dot(chosen, parts_ref[:, : 2 * BAND], preferred_element_type=f32)
    xr, xi = spec[:, :BAND], spec[:, BAND:]
    wr, wi = tspec_ref[:, :BAND], tspec_ref[:, BAND:]
    cross_ref[:, :BAND] = (wr * xr + wi * xi).astype(bf16)
    cross_ref[:, BAND:] = (wr * xi - wi * xr).astype(bf16)
    unsent = (1.0 - jnp.sum(chosen.astype(f32), axis=1, keepdims=True) / 3.0) * EPSILON**-0.5
    step = 2 * LANES
    for c in range(0, LN, step):
        corr = jnp.dot(cross_ref[...], lag_ref[:, c : c + step], preferred_element_type=f32)
        inv = jnp.dot(
            chosen, parts_ref[:, 2 * BAND + c : 2 * BAND + c + step], preferred_element_type=f32
        )
        normed = corr * (inv + unsent) * scale_ref[...]
        for k in range(step // LANES):
            line_ref[pl.ds(c // LANES + k, wide, stride=LN // LANES), :] = normed[
                :, LANES * k : LANES * (k + 1)
            ]

    rows_out = OUT // LANES
    lane4 = lax.broadcasted_iota(jnp.int32, (rows_out, LANES), 1)

    def one_template(t, carry):
        total_score = jnp.zeros((rows_out, LANES), f32)
        used = active_ref[0, t]
        for j in range(slots):
            move = move_ref[t, j]
            q, s = move // LANES, move % LANES
            start = (t * padded + j) * (LN // LANES) + q
            first = line_ref[pl.ds(start, rows_out), :]
            second = line_ref[pl.ds(start + 1, rows_out), :]
            joined = jnp.where(lane4 >= s, first, second)
            turned = pltpu.roll(joined, (LANES - s) % LANES, 1)
            total_score += turned * jnp.where(j < used, 1.0, 0.0)
        sums_ref[pl.ds(t * rows_out, rows_out), :] = total_score
        return carry

    lax.fori_loop(0, templs, one_template, 0)
    for a in range(rows_out):
        out_ref[:, LANES * a : LANES * (a + 1)] = sums_ref[pl.ds(a, templs, stride=rows_out), :]


def on_device(
    geometry, waveforms, templates, channel_ids, moveouts, active, border, border_count
):
    regions, tmpls, subs, offsets = geometry
    devices = tmpls * subs * len(offsets)
    chans = waveforms.shape[1]
    bmax = border.shape[2]
    templs, slots = channel_ids.shape[1:]
    padded = -(-slots // 16) * 16
    wide = templs * padded
    short_table, lag_table = wide_tables()
    pay_rows = -(-(chans * CHUNKS + 3) // 8) * 8
    vmem = pl.BlockSpec(memory_space=pltpu.VMEM)
    smem = pl.BlockSpec(memory_space=pltpu.SMEM)
    f32, bf16 = jnp.float32, jnp.bfloat16
    recv, tspec, scale = pl.pallas_call(
        functools.partial(station_kernel, geometry),
        out_shape=(
            jax.ShapeDtypeStruct((devices, pay_rows, LANES), f32),
            jax.ShapeDtypeStruct((wide, 2 * BAND), f32),
            jax.ShapeDtypeStruct((wide, 1), f32),
        ),
        in_specs=[vmem] * 11,
        out_specs=(vmem, vmem, vmem),
        scratch_shapes=[
            pltpu.VMEM((pay_rows, LANES), f32),
            pltpu.VMEM((RES * chans, LANES), f32),
            pltpu.VMEM((chans, 2 * BAND), f32),
            pltpu.VMEM((templs, padded, K), bf16),
            pltpu.SemaphoreType.DMA((devices,)),
            pltpu.SemaphoreType.DMA((devices,)),
        ],
        compiler_params=pltpu.CompilerParams(collective_id=0, has_side_effects=True),
        name="stations",
    )(
        waveforms[0], border[0], border_count, templates[0], short_table,
        *small_tables(chans),
    )
    scores = pl.pallas_call(
        functools.partial(match_kernel, geometry, chans, bmax),
        out_shape=jax.ShapeDtypeStruct((templs, OUT), f32),
        in_specs=[vmem, vmem, vmem, vmem, smem, smem, vmem],
        out_specs=vmem,
        scratch_shapes=[
            pltpu.VMEM((chans * devices, CHUNKS * LANES), f32),
            pltpu.VMEM((3 * chans * devices, CHUNKS * LANES), bf16),
            pltpu.VMEM((wide, 2 * BAND), bf16),
            pltpu.VMEM((wide * (LN // LANES), LANES), f32),
            pltpu.VMEM((templs * (OUT // LANES), LANES), f32),
        ],
        name="match",
    )(recv, tspec, scale, channel_ids[0], moveouts[0], active, lag_table)
    return scores[None]


def solution(mesh):
    regions, tmpls, subs = (mesh.shape[a] for a in ("region", "tmpl", "sub"))
    offsets = tuple(dict.fromkeys((0, (regions - 1) % regions, 1 % regions)))
    geometry = (regions, tmpls, subs, offsets)
    in_specs = (
        P("region", ("tmpl", "sub"), "groups"),
        P("region", ("tmpl", "sub"), None, None),
        P("region", ("tmpl", "sub"), None),
        P("region", ("tmpl", "sub"), None),
        P("region", ("tmpl", "sub")),
        P("region", None, None),
        P("region", None),
    )
    return jax.shard_map(
        functools.partial(on_device, geometry),
        mesh=mesh,
        in_specs=in_specs,
        out_specs=P("region", ("tmpl", "sub"), "groups"),
        check_vma=False,
    )
```

```python
import functools

import jax
import jax.numpy as jnp
import ml_dtypes
import numpy as np
from jax import lax
from jax.experimental import pallas as pl
from jax.experimental.pallas import tpu as pltpu
from jax.sharding import PartitionSpec as P

NF = 2048
F0 = 40
BAND = 384
K = 400
OUT = 512
LN = 1024
EPSILON = 1e-06

LANES = 128
RES = NF // LANES
STEPS = BAND // RES
CHUNKS = (2 * BAND + LN) // LANES
SPEC_CHUNKS = 2 * BAND // LANES
STATION_INPUTS = 11
MATCH_INPUTS = 7
MESH = pl.DeviceIdType.MESH
HIGH = lax.Precision.HIGHEST


def dot(a, b):
    return jnp.dot(a, b, precision=HIGH, preferred_element_type=jnp.float32)


def bin_order():
    r, g = np.meshgrid(np.arange(RES), np.arange(STEPS), indexing="ij")
    return (F0 + RES * g + r).reshape(-1)


def wide_tables():
    bins = bin_order()
    turn = 2.0 * np.pi / NF
    short = (np.arange(K)[:, None] * bins[None, :] % NF) * turn
    short = np.concatenate([np.cos(short), -np.sin(short)], axis=1)
    lag = (bins[:, None] * np.arange(LN)[None, :] % NF) * turn
    lag = np.concatenate([np.cos(lag), -np.sin(lag)], axis=0)
    as_bf16 = lambda x: x.astype(np.float32).astype(ml_dtypes.bfloat16)
    return as_bf16(short), as_bf16(lag)


def small_tables(chans):
    turn = 2.0 * np.pi / NF
    r, a, b, g = np.arange(RES), np.arange(RES), np.arange(LANES), np.arange(STEPS)
    eye = np.eye(chans)
    alpha = (F0 + r)[:, None] * a[None, :] * LANES % NF * turn
    gather = np.concatenate([np.kron(np.cos(alpha), eye), np.kron(-np.sin(alpha), eye)], axis=0)
    spread = 2.0 / NF * np.concatenate(
        [np.kron(np.cos(alpha.T), eye), np.kron(-np.sin(alpha.T), eye)], axis=1
    )
    theta = np.repeat((F0 + r)[:, None] * b[None, :] % NF * turn, chans, axis=0)
    twiddle = np.concatenate([np.cos(theta), np.sin(theta)], axis=0)
    beta = b[:, None] * g[None, :] * RES % NF * turn
    c, s = np.cos(beta), np.sin(beta)
    fwd = np.zeros((2 * LANES, LANES))
    fwd[:LANES, :STEPS], fwd[:LANES, STEPS : 2 * STEPS] = c, -s
    fwd[LANES:, :STEPS], fwd[LANES:, STEPS : 2 * STEPS] = s, c
    inv = np.zeros((LANES, 2 * LANES))
    inv[:STEPS, :LANES], inv[:STEPS, LANES:] = c.T, s.T
    inv[STEPS : 2 * STEPS, :LANES], inv[STEPS : 2 * STEPS, LANES:] = -s.T, c.T
    rows = []
    for i in (0, 1, 3, 4):
        place = LANES * i + b[:, None] - b[None, :]
        rows.append((place >= 0) & (place < K))
    window = np.concatenate(rows, axis=0)
    return [x.astype(np.float32) for x in (gather, spread, twiddle, fwd, inv, window)]


def station_kernel(geometry, *refs):
    count = STATION_INPUTS
    hbm, (recv_ref, *out_hbm) = refs[:count], refs[count : count + 3]
    (pay_ref, rows_ref, spec_ref), local = refs[count + 3 : count + 6], refs[count + 6 : 2 * count + 6]
    tspec_ref, scale_ref, load_sem, send_sem, recv_sem = refs[2 * count + 6 :]
    loads = [pltpu.make_async_copy(h, v, load_sem.at[i]) for i, (h, v) in enumerate(zip(hbm, local))]
    for load in loads:
        load.start()
    (
        wave_ref, gather_ref, twiddle_ref, fwd_ref, inv_ref, spread_ref, window_ref, border_ref,
        count_ref, tmpl_ref, short_ref,
    ) = local
    regions, tmpls, subs, offsets = geometry
    group = tmpls * subs
    region = lax.axis_index("region")
    place = lax.axis_index("tmpl") * subs + lax.axis_index("sub")
    peers = []
    for block, offset in enumerate(offsets):
        there = lax.rem(region + (regions - offset) % regions, regions)
        for step in range(1 if offset == 0 else 0, group):
            peer = lax.rem(place + step, group)
            device = {"region": there, "tmpl": peer // subs, "sub": lax.rem(peer, subs)}
            peers.append((block, step, peer, device))
    barrier = pltpu.get_barrier_semaphore()
    for _, _, _, device in peers:
        pl.semaphore_signal(barrier, inc=1, device_id=device, device_id_type=MESH)

    chans = wave_ref.shape[0]
    half = RES * chans
    loads[0].wait()
    for a in range(RES):
        rows_ref[chans * a : chans * (a + 1), :] = wave_ref[:, LANES * a : LANES * (a + 1)]
    loads[1].wait()
    y = dot(gather_ref[...], rows_ref[...])
    loads[2].wait()
    cos, sin = twiddle_ref[:half, :], twiddle_ref[half:, :]
    yr, yi = y[:half], y[half:]
    z = jnp.concatenate([yr * cos + yi * sin, yi * cos - yr * sin], axis=1)
    loads[3].wait()
    x = dot(z, fwd_ref[...])
    for r in range(RES):
        piece = x[chans * r : chans * (r + 1), :]
        spec_ref[:, STEPS * r : STEPS * (r + 1)] = piece[:, :STEPS]
        spec_ref[:, BAND + STEPS * r : BAND + STEPS * (r + 1)] = piece[:, STEPS : 2 * STEPS]
    for k in range(SPEC_CHUNKS):
        pay_ref[chans * k : chans * (k + 1), :] = spec_ref[:, LANES * k : LANES * (k + 1)]
    loads[4].wait()
    v = dot(x, inv_ref[...])
    vr, vi = v[:, :LANES], v[:, LANES:]
    u = jnp.concatenate([vr * cos - vi * sin, vr * sin + vi * cos], axis=0)
    loads[5].wait()
    filtered = dot(spread_ref[...], u)
    rows_ref[...] = filtered * filtered
    count = LN // LANES * chans
    near = lambda i: rows_ref[chans * i : chans * i + count, :]
    pieces = jnp.concatenate([near(0), near(1) + near(2), near(3), near(4)], axis=1)
    start = chans * SPEC_CHUNKS
    loads[6].wait()
    pay_ref[start : start + count, :] = dot(pieces, window_ref[...])
    loads[7].wait()
    loads[8].wait()
    bmax = border_ref.shape[1]
    base = chans * CHUNKS
    pay_ref[base:, :] = jnp.zeros((pay_ref.shape[0] - base, LANES), jnp.float32)
    pay_ref[base : base + 1, :bmax] = border_ref[1:2, :].astype(jnp.float32)
    pay_ref[base + 1 : base + 2, :bmax] = border_ref[0:1, :].astype(jnp.float32)
    pay_ref[base + 2 : base + 3, :2] = count_ref[...].astype(jnp.float32)

    pl.semaphore_wait(barrier, len(peers))
    copies = []
    for block, step, peer, device in peers:
        copy = pltpu.make_async_remote_copy(
            src_ref=pay_ref,
            dst_ref=recv_ref.at[block * group + place],
            send_sem=send_sem.at[block * group + step],
            recv_sem=recv_sem.at[block * group + place],
            device_id=device,
            device_id_type=MESH,
        )
        copy.start()
        copies.append(copy)
    stores = [pltpu.make_async_copy(pay_ref, recv_ref.at[place], load_sem.at[0])]
    stores[0].start()

    loads[9].wait()
    loads[10].wait()
    waves = tmpl_ref[...]
    tspec_ref[...] = jnp.dot(waves, short_ref[...], preferred_element_type=jnp.float32)
    wide = waves.astype(jnp.float32)
    power = jnp.sum(wide * wide, axis=1, keepdims=True)
    scale_ref[...] = 2.0 / NF * lax.rsqrt(power + EPSILON)
    for i, (v, h) in enumerate(zip((tspec_ref, scale_ref), out_hbm)):
        stores.append(pltpu.make_async_copy(v, h, load_sem.at[i + 1]))
        stores[-1].start()

    for store in stores:
        store.wait()
    for copy in copies:
        copy.wait_send()
    for block, step, peer, device in peers:
        slot = block * group + peer
        pltpu.make_async_remote_copy(
            src_ref=pay_ref,
            dst_ref=recv_ref.at[slot],
            send_sem=send_sem.at[block * group + step],
            recv_sem=recv_sem.at[slot],
            device_id=device,
            device_id_type=MESH,
        ).wait_recv()


def match_kernel(geometry, chans, bmax, *refs):
    count = MATCH_INPUTS
    hbm, out_ref, local = refs[:count], refs[count], refs[count + 1 : 2 * count + 1]
    table_ref, parts_ref, cross_ref, line_ref, sums_ref, load_sem = refs[2 * count + 1 :]
    loads = [pltpu.make_async_copy(h, v, load_sem.at[i]) for i, (h, v) in enumerate(zip(hbm, local))]
    for load in loads:
        load.start()
    recv_ref, ids_ref, tspec_ref, lag_ref, scale_ref, move_ref, active_ref = local
    regions, tmpls, subs, offsets = geometry
    group = tmpls * subs
    own = group * chans
    total = own * len(offsets)
    ext = own + 2 * bmax
    slots, _, templs = ids_ref.shape
    wide = slots * templs
    bf16, f32 = jnp.bfloat16, jnp.float32

    loads[0].wait()
    for d in range(group * len(offsets)):
        for k in range(CHUNKS):
            table_ref[chans * d : chans * (d + 1), LANES * k : LANES * (k + 1)] = recv_ref[
                d, chans * k : chans * (k + 1), :
            ]
    table_ref[:, 2 * BAND :] = lax.rsqrt(table_ref[:, 2 * BAND :] + EPSILON)
    table = table_ref[...]
    high = table.astype(bf16)
    rest = table - high.astype(f32)
    middle = rest.astype(bf16)
    low = (rest - middle.astype(f32)).astype(bf16)
    parts_ref[...] = jnp.concatenate([high, middle, low], axis=0)

    region = lax.axis_index("region")
    left = offsets.index((regions - 1) % regions)
    right = offsets.index(1 % regions)
    base = chans * CHUNKS
    lane = lax.broadcasted_iota(jnp.int32, (1, LANES), 1)
    info = recv_ref[left * group, base : base + 3, :]
    from_left = info[0:1].astype(jnp.int32)
    left_count = jnp.where(region > 0, info[2:3, 1:2].astype(jnp.int32), 0)
    info = recv_ref[right * group, base : base + 3, :]
    from_right = info[1:2].astype(jnp.int32)
    right_count = jnp.where(region < regions - 1, info[2:3, 0:1].astype(jnp.int32), 0)
    row = lax.broadcasted_iota(jnp.int32, (3 * total, 1), 0) % total
    one = lambda mask: jnp.where(mask, 1.0, 0.0).astype(bf16)
    own_pick = one(row == lane[:, :own])
    left_pick = one((row == left * own + from_left[:, :bmax]) & (lane[:, :bmax] < left_count))
    right_pick = one((row == right * own + from_right[:, :bmax]) & (lane[:, :bmax] < right_count))

    loads[1].wait()
    square = (templs, templs)
    same = lax.broadcasted_iota(jnp.int32, square, 0) == lax.broadcasted_iota(jnp.int32, square, 1)
    ids = jnp.concatenate(
        [
            jnp.sum(jnp.where(same, ids_ref[j], 0), axis=1, keepdims=True, dtype=jnp.int32)
            for j in range(slots)
        ],
        axis=0,
    )
    contract = (((1,), (1,)), ((), ()))
    pick = lambda first, rows_pick: lax.dot_general(
        one(ids == first + lane[:, : rows_pick.shape[1]]), rows_pick, contract,
        preferred_element_type=f32,
    )
    chosen = pick(0, own_pick) + pick(own, left_pick) + pick(own + bmax, right_pick)
    chosen = chosen.astype(bf16)

    spec = jnp.dot(chosen, parts_ref[:, : 2 * BAND], preferred_element_type=f32)
    loads[2].wait()
    xr, xi = spec[:, :BAND], spec[:, BAND:]
    wr, wi = tspec_ref[:, :BAND], tspec_ref[:, BAND:]
    cross_ref[:, :BAND] = (wr * xr + wi * xi).astype(bf16)
    cross_ref[:, BAND:] = (wr * xi - wi * xr).astype(bf16)
    unsent = (1.0 - jnp.sum(chosen.astype(f32), axis=1, keepdims=True) / 3.0) * EPSILON**-0.5
    step = 2 * LANES
    loads[3].wait()
    loads[4].wait()
    for c in range(0, LN, step):
        corr = jnp.dot(cross_ref[...], lag_ref[:, c : c + step], preferred_element_type=f32)
        inv = jnp.dot(
            chosen, parts_ref[:, 2 * BAND + c : 2 * BAND + c + step], preferred_element_type=f32
        )
        normed = corr * (inv + unsent) * scale_ref[...]
        for k in range(step // LANES):
            line_ref[pl.ds(c // LANES + k, wide, stride=LN // LANES), :] = normed[
                :, LANES * k : LANES * (k + 1)
            ]

    loads[5].wait()
    loads[6].wait()
    rows_out = OUT // LANES
    lane4 = lax.broadcasted_iota(jnp.int32, (rows_out, LANES), 1)

    def one_template(t, carry):
        total_score = jnp.zeros((rows_out, LANES), f32)
        used = active_ref[0, t]
        for j in range(slots):
            move = move_ref[j, 0, t]
            q, s = move // LANES, move % LANES
            start = (j * templs + t) * (LN // LANES) + q
            first = line_ref[pl.ds(start, rows_out), :]
            second = line_ref[pl.ds(start + 1, rows_out), :]
            joined = jnp.where(lane4 >= s, first, second)
            turned = pltpu.roll(joined, (LANES - s) % LANES, 1)
            total_score += turned * jnp.where(j < used, 1.0, 0.0)
        sums_ref[pl.ds(t * rows_out, rows_out), :] = total_score
        return carry

    lax.fori_loop(0, templs, one_template, 0)
    for a in range(rows_out):
        out_ref[:, LANES * a : LANES * (a + 1)] = sums_ref[pl.ds(a, templs, stride=rows_out), :]


def on_device(
    geometry, waveforms, templates, channel_ids, moveouts, active, border, border_count
):
    regions, tmpls, subs, offsets = geometry
    devices = tmpls * subs * len(offsets)
    chans = waveforms.shape[1]
    bmax = border.shape[2]
    templs, slots = channel_ids.shape[1:]
    wide = slots * templs
    by_slot = lambda x: jnp.transpose(x, (2, 0, 1))
    short_table, lag_table = wide_tables()
    pay_rows = -(-(chans * CHUNKS + 3) // 8) * 8
    vmem = pl.BlockSpec(memory_space=pltpu.VMEM)
    hbm = pl.BlockSpec(memory_space=pltpu.HBM)
    f32, bf16 = jnp.float32, jnp.bfloat16
    gather, spread, twiddle, fwd, inv, window = small_tables(chans)
    rows = jnp.swapaxes(templates[0], 0, 1).reshape(wide, K)
    inputs = (
        waveforms[0], gather, twiddle, fwd, inv, spread, window, border[0], border_count, rows,
        short_table,
    )
    recv, tspec, scale = pl.pallas_call(
        functools.partial(station_kernel, geometry),
        out_shape=(
            jax.ShapeDtypeStruct((devices, pay_rows, LANES), f32),
            jax.ShapeDtypeStruct((wide, 2 * BAND), f32),
            jax.ShapeDtypeStruct((wide, 1), f32),
        ),
        in_specs=[hbm] * STATION_INPUTS,
        out_specs=(hbm, hbm, hbm),
        scratch_shapes=[
            pltpu.VMEM((pay_rows, LANES), f32),
            pltpu.VMEM((RES * chans, LANES), f32),
            pltpu.VMEM((chans, 2 * BAND), f32),
            *[pltpu.VMEM(x.shape, x.dtype) for x in inputs],
            pltpu.VMEM((wide, 2 * BAND), f32),
            pltpu.VMEM((wide, 1), f32),
            pltpu.SemaphoreType.DMA((STATION_INPUTS,)),
            pltpu.SemaphoreType.DMA((devices,)),
            pltpu.SemaphoreType.DMA((devices,)),
        ],
        compiler_params=pltpu.CompilerParams(collective_id=0, has_side_effects=True),
        name="stations",
    )(*inputs)
    inputs = (recv, by_slot(channel_ids), tspec, lag_table, scale, by_slot(moveouts), active)
    spaces = [pltpu.VMEM] * 5 + [pltpu.SMEM] * 2
    scores = pl.pallas_call(
        functools.partial(match_kernel, geometry, chans, bmax),
        out_shape=jax.ShapeDtypeStruct((templs, OUT), f32),
        in_specs=[hbm] * MATCH_INPUTS,
        out_specs=vmem,
        scratch_shapes=[
            *[space(x.shape, x.dtype) for space, x in zip(spaces, inputs)],
            pltpu.VMEM((chans * devices, CHUNKS * LANES), f32),
            pltpu.VMEM((3 * chans * devices, CHUNKS * LANES), bf16),
            pltpu.VMEM((wide, 2 * BAND), bf16),
            pltpu.VMEM((wide * (LN // LANES), LANES), f32),
            pltpu.VMEM((templs * (OUT // LANES), LANES), f32),
            pltpu.SemaphoreType.DMA((MATCH_INPUTS,)),
        ],
        name="match",
    )(*inputs)
    return scores[None]


def solution(mesh):
    regions, tmpls, subs = (mesh.shape[a] for a in ("region", "tmpl", "sub"))
    offsets = tuple(dict.fromkeys((0, (regions - 1) % regions, 1 % regions)))
    geometry = (regions, tmpls, subs, offsets)
    in_specs = (
        P("region", ("tmpl", "sub"), "groups"),
        P("region", ("tmpl", "sub"), None, None),
        P("region", ("tmpl", "sub"), None),
        P("region", ("tmpl", "sub"), None),
        P("region", ("tmpl", "sub")),
        P("region", None, None),
        P("region", None),
    )
    return jax.shard_map(
        functools.partial(on_device, geometry),
        mesh=mesh,
        in_specs=in_specs,
        out_specs=P("region", ("tmpl", "sub"), "groups"),
        check_vma=False,
    )
```

```python
import functools

import jax
import jax.numpy as jnp
import ml_dtypes
import numpy as np
from jax import lax
from jax.experimental import pallas as pl
from jax.experimental.pallas import tpu as pltpu
from jax.sharding import PartitionSpec as P

NF = 2048
F0 = 40
BAND = 384
K = 400
OUT = 512
LN = 1024
EPSILON = 1e-06

LANES = 128
RES = NF // LANES
STEPS = BAND // RES
CHUNKS = (2 * BAND + LN) // LANES
SPEC_CHUNKS = 2 * BAND // LANES
STATION_INPUTS = 11
MATCH_INPUTS = 7
MESH = pl.DeviceIdType.MESH
HIGH = lax.Precision.HIGHEST


def dot(a, b):
    return jnp.dot(a, b, precision=HIGH, preferred_element_type=jnp.float32)


def bin_order():
    r, g = np.meshgrid(np.arange(RES), np.arange(STEPS), indexing="ij")
    return (F0 + RES * g + r).reshape(-1)


def wide_tables():
    bins = bin_order()
    turn = 2.0 * np.pi / NF
    short = (np.arange(K)[:, None] * bins[None, :] % NF) * turn
    short = np.concatenate([np.cos(short), -np.sin(short)], axis=1)
    lag = (bins[:, None] * np.arange(LN)[None, :] % NF) * turn
    lag = np.concatenate([np.cos(lag), -np.sin(lag)], axis=0)
    as_bf16 = lambda x: x.astype(np.float32).astype(ml_dtypes.bfloat16)
    return as_bf16(short), as_bf16(lag)


def small_tables(chans):
    turn = 2.0 * np.pi / NF
    r, a, b, g = np.arange(RES), np.arange(RES), np.arange(LANES), np.arange(STEPS)
    eye = np.eye(chans)
    alpha = (F0 + r)[:, None] * a[None, :] * LANES % NF * turn
    gather = np.concatenate([np.kron(np.cos(alpha), eye), np.kron(-np.sin(alpha), eye)], axis=0)
    spread = 2.0 / NF * np.concatenate(
        [np.kron(np.cos(alpha.T), eye), np.kron(-np.sin(alpha.T), eye)], axis=1
    )
    theta = np.repeat((F0 + r)[:, None] * b[None, :] % NF * turn, chans, axis=0)
    twiddle = np.concatenate([np.cos(theta), np.sin(theta)], axis=0)
    beta = b[:, None] * g[None, :] * RES % NF * turn
    c, s = np.cos(beta), np.sin(beta)
    fwd = np.zeros((2 * LANES, LANES))
    fwd[:LANES, :STEPS], fwd[:LANES, STEPS : 2 * STEPS] = c, -s
    fwd[LANES:, :STEPS], fwd[LANES:, STEPS : 2 * STEPS] = s, c
    inv = np.zeros((LANES, 2 * LANES))
    inv[:STEPS, :LANES], inv[:STEPS, LANES:] = c.T, s.T
    inv[STEPS : 2 * STEPS, :LANES], inv[STEPS : 2 * STEPS, LANES:] = -s.T, c.T
    rows = []
    for i in (0, 1, 3, 4):
        place = LANES * i + b[:, None] - b[None, :]
        rows.append((place >= 0) & (place < K))
    window = np.concatenate(rows, axis=0)
    return [x.astype(np.float32) for x in (gather, spread, twiddle, fwd, inv, window)]


def station_kernel(geometry, *refs):
    count = STATION_INPUTS
    hbm, (recv_ref, *out_hbm) = refs[:count], refs[count : count + 3]
    (pay_ref, rows_ref, spec_ref), local = refs[count + 3 : count + 6], refs[count + 6 : 2 * count + 6]
    tspec_ref, scale_ref, load_sem, send_sem, recv_sem = refs[2 * count + 6 :]
    loads = [pltpu.make_async_copy(h, v, load_sem.at[i]) for i, (h, v) in enumerate(zip(hbm, local))]
    for load in loads:
        load.start()
    (
        wave_ref, gather_ref, twiddle_ref, fwd_ref, inv_ref, spread_ref, window_ref, border_ref,
        count_ref, tmpl_ref, short_ref,
    ) = local
    regions, tmpls, subs, offsets = geometry
    group = tmpls * subs
    region = lax.axis_index("region")
    place = lax.axis_index("tmpl") * subs + lax.axis_index("sub")
    tmpl, sub = lax.axis_index("tmpl"), lax.axis_index("sub")
    peers = []
    for block, offset in enumerate(offsets):
        there = lax.rem(region + (regions - offset) % regions, regions)
        for step in range(1 if offset == 0 else 0, tmpls):
            peer = lax.rem(tmpl + step, tmpls)
            peers.append((block, peer * subs + sub, {"region": there, "tmpl": peer, "sub": sub}))
    mates = [lax.rem(sub + step, subs) for step in range(1, subs)]

    def copy_to(slot, source, device, lane):
        return pltpu.make_async_remote_copy(
            src_ref=source,
            dst_ref=recv_ref.at[slot],
            send_sem=send_sem.at[lane],
            recv_sem=recv_sem.at[slot],
            device_id=device,
            device_id_type=MESH,
        )

    barrier = pltpu.get_barrier_semaphore()
    for device in [device for _, _, device in peers] + [{"sub": mate} for mate in mates]:
        pl.semaphore_signal(barrier, inc=1, device_id=device, device_id_type=MESH)

    chans = wave_ref.shape[0]
    half = RES * chans
    loads[0].wait()
    for a in range(RES):
        rows_ref[chans * a : chans * (a + 1), :] = wave_ref[:, LANES * a : LANES * (a + 1)]
    loads[1].wait()
    y = dot(gather_ref[...], rows_ref[...])
    loads[2].wait()
    cos, sin = twiddle_ref[:half, :], twiddle_ref[half:, :]
    yr, yi = y[:half], y[half:]
    z = jnp.concatenate([yr * cos + yi * sin, yi * cos - yr * sin], axis=1)
    loads[3].wait()
    x = dot(z, fwd_ref[...])
    for r in range(RES):
        piece = x[chans * r : chans * (r + 1), :]
        spec_ref[:, STEPS * r : STEPS * (r + 1)] = piece[:, :STEPS]
        spec_ref[:, BAND + STEPS * r : BAND + STEPS * (r + 1)] = piece[:, STEPS : 2 * STEPS]
    for k in range(SPEC_CHUNKS):
        pay_ref[chans * k : chans * (k + 1), :] = spec_ref[:, LANES * k : LANES * (k + 1)]
    loads[4].wait()
    v = dot(x, inv_ref[...])
    vr, vi = v[:, :LANES], v[:, LANES:]
    u = jnp.concatenate([vr * cos - vi * sin, vr * sin + vi * cos], axis=0)
    loads[5].wait()
    filtered = dot(spread_ref[...], u)
    rows_ref[...] = filtered * filtered
    count = LN // LANES * chans
    near = lambda i: rows_ref[chans * i : chans * i + count, :]
    pieces = jnp.concatenate([near(0), near(1) + near(2), near(3), near(4)], axis=1)
    start = chans * SPEC_CHUNKS
    loads[6].wait()
    pay_ref[start : start + count, :] = dot(pieces, window_ref[...])
    loads[7].wait()
    loads[8].wait()
    bmax = border_ref.shape[1]
    base = chans * CHUNKS
    pay_ref[base:, :] = jnp.zeros((pay_ref.shape[0] - base, LANES), jnp.float32)
    pay_ref[base : base + 1, :bmax] = border_ref[1:2, :].astype(jnp.float32)
    pay_ref[base + 1 : base + 2, :bmax] = border_ref[0:1, :].astype(jnp.float32)
    pay_ref[base + 2 : base + 3, :2] = count_ref[...].astype(jnp.float32)

    pl.semaphore_wait(barrier, len(peers) + len(mates))
    copies = []

    def send(slot, source, device):
        copies.append(copy_to(slot, source, device, len(copies)))
        copies[-1].start()

    for block, peer, device in reversed(peers):
        send(block * group + place, pay_ref, device)
    for mate in mates:
        send(place, pay_ref, {"sub": mate})
    stores = [pltpu.make_async_copy(pay_ref, recv_ref.at[place], load_sem.at[0])]
    stores[0].start()

    loads[9].wait()
    loads[10].wait()
    waves = tmpl_ref[...]
    tspec_ref[...] = jnp.dot(waves, short_ref[...], preferred_element_type=jnp.float32)
    wide = waves.astype(jnp.float32)
    power = jnp.sum(wide * wide, axis=1, keepdims=True)
    scale_ref[...] = 2.0 / NF * lax.rsqrt(power + EPSILON)
    for i, (v, h) in enumerate(zip((tspec_ref, scale_ref), out_hbm)):
        stores.append(pltpu.make_async_copy(v, h, load_sem.at[i + 1]))
        stores[-1].start()

    for store in stores:
        store.wait()
    for block, peer, device in peers:
        slot = block * group + peer
        copy_to(slot, pay_ref, device, 0).wait_recv()
        for mate in mates:
            send(slot, recv_ref.at[slot], {"sub": mate})
    for mate in mates:
        for block in range(len(offsets)):
            for step in range(tmpls):
                slot = block * group + lax.rem(tmpl + step, tmpls) * subs + mate
                copy_to(slot, pay_ref, {"sub": mate}, 0).wait_recv()
    for copy in copies:
        copy.wait_send()


def match_kernel(geometry, chans, bmax, *refs):
    count = MATCH_INPUTS
    hbm, out_ref, local = refs[:count], refs[count], refs[count + 1 : 2 * count + 1]
    table_ref, parts_ref, cross_ref, line_ref, sums_ref, load_sem = refs[2 * count + 1 :]
    loads = [pltpu.make_async_copy(h, v, load_sem.at[i]) for i, (h, v) in enumerate(zip(hbm, local))]
    for load in loads:
        load.start()
    recv_ref, ids_ref, tspec_ref, lag_ref, scale_ref, move_ref, active_ref = local
    regions, tmpls, subs, offsets = geometry
    group = tmpls * subs
    own = group * chans
    total = own * len(offsets)
    ext = own + 2 * bmax
    slots, _, templs = ids_ref.shape
    wide = slots * templs
    bf16, f32 = jnp.bfloat16, jnp.float32

    loads[0].wait()
    for d in range(group * len(offsets)):
        for k in range(CHUNKS):
            table_ref[chans * d : chans * (d + 1), LANES * k : LANES * (k + 1)] = recv_ref[
                d, chans * k : chans * (k + 1), :
            ]
    table_ref[:, 2 * BAND :] = lax.rsqrt(table_ref[:, 2 * BAND :] + EPSILON)
    table = table_ref[...]
    high = table.astype(bf16)
    rest = table - high.astype(f32)
    middle = rest.astype(bf16)
    low = (rest - middle.astype(f32)).astype(bf16)
    parts_ref[...] = jnp.concatenate([high, middle, low], axis=0)

    region = lax.axis_index("region")
    left = offsets.index((regions - 1) % regions)
    right = offsets.index(1 % regions)
    base = chans * CHUNKS
    lane = lax.broadcasted_iota(jnp.int32, (1, LANES), 1)
    info = recv_ref[left * group, base : base + 3, :]
    from_left = info[0:1].astype(jnp.int32)
    left_count = jnp.where(region > 0, info[2:3, 1:2].astype(jnp.int32), 0)
    info = recv_ref[right * group, base : base + 3, :]
    from_right = info[1:2].astype(jnp.int32)
    right_count = jnp.where(region < regions - 1, info[2:3, 0:1].astype(jnp.int32), 0)
    row = lax.broadcasted_iota(jnp.int32, (3 * total, 1), 0) % total
    one = lambda mask: jnp.where(mask, 1.0, 0.0).astype(bf16)
    own_pick = one(row == lane[:, :own])
    left_pick = one((row == left * own + from_left[:, :bmax]) & (lane[:, :bmax] < left_count))
    right_pick = one((row == right * own + from_right[:, :bmax]) & (lane[:, :bmax] < right_count))

    loads[1].wait()
    square = (templs, templs)
    same = lax.broadcasted_iota(jnp.int32, square, 0) == lax.broadcasted_iota(jnp.int32, square, 1)
    ids = jnp.concatenate(
        [
            jnp.sum(jnp.where(same, ids_ref[j], 0), axis=1, keepdims=True, dtype=jnp.int32)
            for j in range(slots)
        ],
        axis=0,
    )
    contract = (((1,), (1,)), ((), ()))
    pick = lambda first, rows_pick: lax.dot_general(
        one(ids == first + lane[:, : rows_pick.shape[1]]), rows_pick, contract,
        preferred_element_type=f32,
    )
    chosen = pick(0, own_pick) + pick(own, left_pick) + pick(own + bmax, right_pick)
    chosen = chosen.astype(bf16)

    spec = jnp.dot(chosen, parts_ref[:, : 2 * BAND], preferred_element_type=f32)
    loads[2].wait()
    xr, xi = spec[:, :BAND], spec[:, BAND:]
    wr, wi = tspec_ref[:, :BAND], tspec_ref[:, BAND:]
    cross_ref[:, :BAND] = (wr * xr + wi * xi).astype(bf16)
    cross_ref[:, BAND:] = (wr * xi - wi * xr).astype(bf16)
    unsent = (1.0 - jnp.sum(chosen.astype(f32), axis=1, keepdims=True) / 3.0) * EPSILON**-0.5
    step = 2 * LANES
    loads[3].wait()
    loads[4].wait()
    for c in range(0, LN, step):
        corr = jnp.dot(cross_ref[...], lag_ref[:, c : c + step], preferred_element_type=f32)
        inv = jnp.dot(
            chosen, parts_ref[:, 2 * BAND + c : 2 * BAND + c + step], preferred_element_type=f32
        )
        normed = corr * (inv + unsent) * scale_ref[...]
        for k in range(step // LANES):
            line_ref[pl.ds(c // LANES + k, wide, stride=LN // LANES), :] = normed[
                :, LANES * k : LANES * (k + 1)
            ]

    loads[5].wait()
    loads[6].wait()
    rows_out = OUT // LANES
    lane4 = lax.broadcasted_iota(jnp.int32, (rows_out, LANES), 1)

    def one_template(t, carry):
        total_score = jnp.zeros((rows_out, LANES), f32)
        used = active_ref[0, t]
        for j in range(slots):
            move = move_ref[j, 0, t]
            q, s = move >> 7, move & (LANES - 1)
            start = (j * templs + t) * (LN // LANES) + q
            first = line_ref[pl.ds(start, rows_out), :]
            second = line_ref[pl.ds(start + 1, rows_out), :]
            joined = jnp.where(lane4 >= s, first, second)
            turned = pltpu.roll(joined, (LANES - s) & (LANES - 1), 1)
            total_score += turned * jnp.where(j < used, 1.0, 0.0)
        sums_ref[pl.ds(t * rows_out, rows_out), :] = total_score
        return carry

    lax.fori_loop(0, templs, one_template, 0, unroll=8)
    for a in range(rows_out):
        out_ref[:, LANES * a : LANES * (a + 1)] = sums_ref[pl.ds(a, templs, stride=rows_out), :]


def on_device(
    geometry, waveforms, templates, channel_ids, moveouts, active, border, border_count
):
    regions, tmpls, subs, offsets = geometry
    devices = tmpls * subs * len(offsets)
    chans = waveforms.shape[1]
    bmax = border.shape[2]
    templs, slots = channel_ids.shape[1:]
    wide = slots * templs
    by_slot = lambda x: jnp.transpose(x, (2, 0, 1))
    short_table, lag_table = wide_tables()
    pay_rows = -(-(chans * CHUNKS + 3) // 8) * 8
    vmem = pl.BlockSpec(memory_space=pltpu.VMEM)
    hbm = pl.BlockSpec(memory_space=pltpu.HBM)
    f32, bf16 = jnp.float32, jnp.bfloat16
    gather, spread, twiddle, fwd, inv, window = small_tables(chans)
    rows = jnp.swapaxes(templates[0], 0, 1).reshape(wide, K)
    inputs = (
        waveforms[0], gather, twiddle, fwd, inv, spread, window, border[0], border_count, rows,
        short_table,
    )
    recv, tspec, scale = pl.pallas_call(
        functools.partial(station_kernel, geometry),
        out_shape=(
            jax.ShapeDtypeStruct((devices, pay_rows, LANES), f32),
            jax.ShapeDtypeStruct((wide, 2 * BAND), f32),
            jax.ShapeDtypeStruct((wide, 1), f32),
        ),
        in_specs=[hbm] * STATION_INPUTS,
        out_specs=(hbm, hbm, hbm),
        scratch_shapes=[
            pltpu.VMEM((pay_rows, LANES), f32),
            pltpu.VMEM((RES * chans, LANES), f32),
            pltpu.VMEM((chans, 2 * BAND), f32),
            *[pltpu.VMEM(x.shape, x.dtype) for x in inputs],
            pltpu.VMEM((wide, 2 * BAND), f32),
            pltpu.VMEM((wide, 1), f32),
            pltpu.SemaphoreType.DMA((STATION_INPUTS,)),
            pltpu.SemaphoreType.DMA((devices,)),
            pltpu.SemaphoreType.DMA((devices,)),
        ],
        compiler_params=pltpu.CompilerParams(collective_id=0, has_side_effects=True),
        name="stations",
    )(*inputs)
    inputs = (recv, by_slot(channel_ids), tspec, lag_table, scale, by_slot(moveouts), active)
    spaces = [pltpu.VMEM] * 5 + [pltpu.SMEM] * 2
    scores = pl.pallas_call(
        functools.partial(match_kernel, geometry, chans, bmax),
        out_shape=jax.ShapeDtypeStruct((templs, OUT), f32),
        in_specs=[hbm] * MATCH_INPUTS,
        out_specs=vmem,
        scratch_shapes=[
            *[space(x.shape, x.dtype) for space, x in zip(spaces, inputs)],
            pltpu.VMEM((chans * devices, CHUNKS * LANES), f32),
            pltpu.VMEM((3 * chans * devices, CHUNKS * LANES), bf16),
            pltpu.VMEM((wide, 2 * BAND), bf16),
            pltpu.VMEM((wide * (LN // LANES), LANES), f32),
            pltpu.VMEM((templs * (OUT // LANES), LANES), f32),
            pltpu.SemaphoreType.DMA((MATCH_INPUTS,)),
        ],
        name="match",
    )(*inputs)
    return scores[None]


def solution(mesh):
    regions, tmpls, subs = (mesh.shape[a] for a in ("region", "tmpl", "sub"))
    offsets = tuple(dict.fromkeys((0, (regions - 1) % regions, 1 % regions)))
    geometry = (regions, tmpls, subs, offsets)
    in_specs = (
        P("region", ("tmpl", "sub"), "groups"),
        P("region", ("tmpl", "sub"), None, None),
        P("region", ("tmpl", "sub"), None),
        P("region", ("tmpl", "sub"), None),
        P("region", ("tmpl", "sub")),
        P("region", None, None),
        P("region", None),
    )
    return jax.shard_map(
        functools.partial(on_device, geometry),
        mesh=mesh,
        in_specs=in_specs,
        out_specs=P("region", ("tmpl", "sub"), "groups"),
        check_vma=False,
    )
```

```python
import functools

import jax
import jax.numpy as jnp
import ml_dtypes
import numpy as np
from jax import lax
from jax.experimental import pallas as pl
from jax.experimental.pallas import tpu as pltpu
from jax.sharding import PartitionSpec as P

NF = 2048
F0 = 40
BAND = 384
K = 400
OUT = 512
LN = 1024
EPSILON = 1e-06

LANES = 128
RES = NF // LANES
STEPS = BAND // RES
CHUNKS = (2 * BAND + LN) // LANES
SPEC_CHUNKS = 2 * BAND // LANES
STATION_INPUTS = 11
MATCH_INPUTS = 7
MESH = pl.DeviceIdType.MESH
HIGH = lax.Precision.HIGHEST


def dot(a, b):
    return jnp.dot(a, b, precision=HIGH, preferred_element_type=jnp.float32)


def bin_order():
    r, g = np.meshgrid(np.arange(RES), np.arange(STEPS), indexing="ij")
    return (F0 + RES * g + r).reshape(-1)


def wide_tables():
    bins = bin_order()
    turn = 2.0 * np.pi / NF
    short = (np.arange(K)[:, None] * bins[None, :] % NF) * turn
    short = np.concatenate([np.cos(short), -np.sin(short)], axis=1)
    lag = (bins[:, None] * np.arange(LN)[None, :] % NF) * turn
    lag = np.concatenate([np.cos(lag), -np.sin(lag)], axis=0)
    as_bf16 = lambda x: x.astype(np.float32).astype(ml_dtypes.bfloat16)
    return as_bf16(short), as_bf16(lag)


def small_tables(chans):
    turn = 2.0 * np.pi / NF
    r, a, b, g = np.arange(RES), np.arange(RES), np.arange(LANES), np.arange(STEPS)
    eye = np.eye(chans)
    alpha = (F0 + r)[:, None] * a[None, :] * LANES % NF * turn
    gather = np.concatenate([np.kron(np.cos(alpha), eye), np.kron(-np.sin(alpha), eye)], axis=0)
    spread = 2.0 / NF * np.concatenate(
        [np.kron(np.cos(alpha.T), eye), np.kron(-np.sin(alpha.T), eye)], axis=1
    )
    theta = np.repeat((F0 + r)[:, None] * b[None, :] % NF * turn, chans, axis=0)
    twiddle = np.concatenate([np.cos(theta), np.sin(theta)], axis=0)
    beta = b[:, None] * g[None, :] * RES % NF * turn
    c, s = np.cos(beta), np.sin(beta)
    fwd = np.zeros((2 * LANES, LANES))
    fwd[:LANES, :STEPS], fwd[:LANES, STEPS : 2 * STEPS] = c, -s
    fwd[LANES:, :STEPS], fwd[LANES:, STEPS : 2 * STEPS] = s, c
    inv = np.zeros((LANES, 2 * LANES))
    inv[:STEPS, :LANES], inv[:STEPS, LANES:] = c.T, s.T
    inv[STEPS : 2 * STEPS, :LANES], inv[STEPS : 2 * STEPS, LANES:] = -s.T, c.T
    rows = []
    for i in (0, 1, 3, 4):
        place = LANES * i + b[:, None] - b[None, :]
        rows.append((place >= 0) & (place < K))
    window = np.concatenate(rows, axis=0)
    tables = [x.astype(np.float32) for x in (gather, spread, twiddle, fwd, inv)]
    return tables + [window.astype(np.float32).astype(ml_dtypes.bfloat16)]


def station_kernel(geometry, *refs):
    count = STATION_INPUTS
    hbm, (recv_ref, *out_hbm) = refs[:count], refs[count : count + 3]
    (pay_ref, rows_ref, spec_ref), local = refs[count + 3 : count + 6], refs[count + 6 : 2 * count + 6]
    tspec_ref, scale_ref, load_sem, send_sem, recv_sem = refs[2 * count + 6 :]
    loads = [pltpu.make_async_copy(h, v, load_sem.at[i]) for i, (h, v) in enumerate(zip(hbm, local))]
    for load in loads:
        load.start()
    (
        wave_ref, gather_ref, twiddle_ref, fwd_ref, inv_ref, spread_ref, window_ref, border_ref,
        count_ref, tmpl_ref, short_ref,
    ) = local
    regions, tmpls, subs, offsets = geometry
    group = tmpls * subs
    region = lax.axis_index("region")
    place = lax.axis_index("tmpl") * subs + lax.axis_index("sub")
    tmpl, sub = lax.axis_index("tmpl"), lax.axis_index("sub")
    peers = []
    for block, offset in enumerate(offsets):
        there = lax.rem(region + (regions - offset) % regions, regions)
        for step in range(1 if offset == 0 else 0, tmpls):
            peer = lax.rem(tmpl + step, tmpls)
            peers.append((block, peer * subs + sub, {"region": there, "tmpl": peer, "sub": sub}))
    mates = [lax.rem(sub + step, subs) for step in range(1, subs)]

    def copy_to(slot, source, device, lane):
        return pltpu.make_async_remote_copy(
            src_ref=source,
            dst_ref=recv_ref.at[slot],
            send_sem=send_sem.at[lane],
            recv_sem=recv_sem.at[slot],
            device_id=device,
            device_id_type=MESH,
        )

    barrier = pltpu.get_barrier_semaphore()
    for device in [device for _, _, device in peers] + [{"sub": mate} for mate in mates]:
        pl.semaphore_signal(barrier, inc=1, device_id=device, device_id_type=MESH)

    chans = wave_ref.shape[0]
    half = RES * chans
    loads[0].wait()
    for a in range(RES):
        rows_ref[chans * a : chans * (a + 1), :] = wave_ref[:, LANES * a : LANES * (a + 1)]
    loads[1].wait()
    y = dot(gather_ref[...], rows_ref[...])
    loads[2].wait()
    cos, sin = twiddle_ref[:half, :], twiddle_ref[half:, :]
    yr, yi = y[:half], y[half:]
    z = jnp.concatenate([yr * cos + yi * sin, yi * cos - yr * sin], axis=1)
    loads[3].wait()
    x = dot(z, fwd_ref[...])
    for r in range(RES):
        piece = x[chans * r : chans * (r + 1), :]
        spec_ref[:, STEPS * r : STEPS * (r + 1)] = piece[:, :STEPS]
        spec_ref[:, BAND + STEPS * r : BAND + STEPS * (r + 1)] = piece[:, STEPS : 2 * STEPS]
    for k in range(SPEC_CHUNKS):
        pay_ref[chans * k : chans * (k + 1), :] = spec_ref[:, LANES * k : LANES * (k + 1)]
    loads[4].wait()
    v = dot(x, inv_ref[...])
    vr, vi = v[:, :LANES], v[:, LANES:]
    u = jnp.concatenate([vr * cos - vi * sin, vr * sin + vi * cos], axis=0)
    loads[5].wait()
    filtered = dot(spread_ref[...], u)
    rows_ref[...] = filtered * filtered
    count = LN // LANES * chans
    near = lambda i: rows_ref[chans * i : chans * i + count, :]
    pieces = jnp.concatenate([near(0), near(1) + near(2), near(3), near(4)], axis=1)
    start = chans * SPEC_CHUNKS
    loads[6].wait()
    high = pieces.astype(jnp.bfloat16)
    rest = pieces - high.astype(jnp.float32)
    middle = rest.astype(jnp.bfloat16)
    low = (rest - middle.astype(jnp.float32)).astype(jnp.bfloat16)
    stacked = jnp.concatenate([high, middle, low], axis=0)
    sums = jnp.dot(stacked, window_ref[...], preferred_element_type=jnp.float32)
    energy = sums[:count] + (sums[count : 2 * count] + sums[2 * count :])
    pay_ref[start : start + count, :] = energy
    loads[7].wait()
    loads[8].wait()
    bmax = border_ref.shape[1]
    base = chans * CHUNKS
    pay_ref[base:, :] = jnp.zeros((pay_ref.shape[0] - base, LANES), jnp.float32)
    pay_ref[base : base + 1, :bmax] = border_ref[1:2, :].astype(jnp.float32)
    pay_ref[base + 1 : base + 2, :bmax] = border_ref[0:1, :].astype(jnp.float32)
    pay_ref[base + 2 : base + 3, :2] = count_ref[...].astype(jnp.float32)

    pl.semaphore_wait(barrier, len(peers) + len(mates))
    copies = []

    def send(slot, source, device):
        copies.append(copy_to(slot, source, device, len(copies)))
        copies[-1].start()

    for block, peer, device in reversed(peers):
        send(block * group + place, pay_ref, device)
    for mate in mates:
        send(place, pay_ref, {"sub": mate})
    stores = [pltpu.make_async_copy(pay_ref, recv_ref.at[place], load_sem.at[0])]
    stores[0].start()

    loads[9].wait()
    loads[10].wait()
    waves = tmpl_ref[...]
    tspec_ref[...] = jnp.dot(waves, short_ref[...], preferred_element_type=jnp.float32)
    wide = waves.astype(jnp.float32)
    power = jnp.sum(wide * wide, axis=1, keepdims=True)
    scale_ref[...] = 2.0 / NF * lax.rsqrt(power + EPSILON)
    for i, (v, h) in enumerate(zip((tspec_ref, scale_ref), out_hbm)):
        stores.append(pltpu.make_async_copy(v, h, load_sem.at[i + 1]))
        stores[-1].start()

    for store in stores:
        store.wait()
    for block, peer, device in peers:
        slot = block * group + peer
        copy_to(slot, pay_ref, device, 0).wait_recv()
        for mate in mates:
            send(slot, recv_ref.at[slot], {"sub": mate})
    for mate in mates:
        for block in range(len(offsets)):
            for step in range(tmpls):
                slot = block * group + lax.rem(tmpl + step, tmpls) * subs + mate
                copy_to(slot, pay_ref, {"sub": mate}, 0).wait_recv()
    for copy in copies:
        copy.wait_send()


def match_kernel(geometry, chans, bmax, *refs):
    count = MATCH_INPUTS
    hbm, out_ref, local = refs[:count], refs[count], refs[count + 1 : 2 * count + 1]
    table_ref, parts_ref, cross_ref, line_ref, sums_ref, load_sem = refs[2 * count + 1 :]
    loads = [pltpu.make_async_copy(h, v, load_sem.at[i]) for i, (h, v) in enumerate(zip(hbm, local))]
    for load in loads:
        load.start()
    recv_ref, ids_ref, tspec_ref, lag_ref, scale_ref, move_ref, active_ref = local
    regions, tmpls, subs, offsets = geometry
    group = tmpls * subs
    own = group * chans
    total = own * len(offsets)
    ext = own + 2 * bmax
    slots, _, templs = ids_ref.shape
    wide = slots * templs
    bf16, f32 = jnp.bfloat16, jnp.float32

    loads[0].wait()
    for d in range(group * len(offsets)):
        for k in range(CHUNKS):
            table_ref[chans * d : chans * (d + 1), LANES * k : LANES * (k + 1)] = recv_ref[
                d, chans * k : chans * (k + 1), :
            ]
    table_ref[:, 2 * BAND :] = lax.rsqrt(table_ref[:, 2 * BAND :] + EPSILON)
    table = table_ref[...]
    high = table.astype(bf16)
    rest = table - high.astype(f32)
    middle = rest.astype(bf16)
    low = (rest - middle.astype(f32)).astype(bf16)
    parts_ref[...] = jnp.concatenate([high, middle, low], axis=0)

    region = lax.axis_index("region")
    left = offsets.index((regions - 1) % regions)
    right = offsets.index(1 % regions)
    base = chans * CHUNKS
    lane = lax.broadcasted_iota(jnp.int32, (1, LANES), 1)
    info = recv_ref[left * group, base : base + 3, :]
    from_left = info[0:1].astype(jnp.int32)
    left_count = jnp.where(region > 0, info[2:3, 1:2].astype(jnp.int32), 0)
    info = recv_ref[right * group, base : base + 3, :]
    from_right = info[1:2].astype(jnp.int32)
    right_count = jnp.where(region < regions - 1, info[2:3, 0:1].astype(jnp.int32), 0)
    row = lax.broadcasted_iota(jnp.int32, (3 * total, 1), 0) % total
    one = lambda mask: jnp.where(mask, 1.0, 0.0).astype(bf16)
    own_pick = one(row == lane[:, :own])
    left_pick = one((row == left * own + from_left[:, :bmax]) & (lane[:, :bmax] < left_count))
    right_pick = one((row == right * own + from_right[:, :bmax]) & (lane[:, :bmax] < right_count))

    loads[1].wait()
    square = (templs, templs)
    same = lax.broadcasted_iota(jnp.int32, square, 0) == lax.broadcasted_iota(jnp.int32, square, 1)
    ids = jnp.concatenate(
        [
            jnp.sum(jnp.where(same, ids_ref[j], 0), axis=1, keepdims=True, dtype=jnp.int32)
            for j in range(slots)
        ],
        axis=0,
    )
    contract = (((1,), (1,)), ((), ()))
    pick = lambda first, rows_pick: lax.dot_general(
        one(ids == first + lane[:, : rows_pick.shape[1]]), rows_pick, contract,
        preferred_element_type=f32,
    )
    chosen = pick(0, own_pick) + pick(own, left_pick) + pick(own + bmax, right_pick)
    chosen = chosen.astype(bf16)

    spec = jnp.dot(chosen, parts_ref[:, : 2 * BAND], preferred_element_type=f32)
    loads[2].wait()
    xr, xi = spec[:, :BAND], spec[:, BAND:]
    wr, wi = tspec_ref[:, :BAND], tspec_ref[:, BAND:]
    cross_ref[:, :BAND] = (wr * xr + wi * xi).astype(bf16)
    cross_ref[:, BAND:] = (wr * xi - wi * xr).astype(bf16)
    unsent = (1.0 - jnp.sum(chosen.astype(f32), axis=1, keepdims=True) / 3.0) * EPSILON**-0.5
    step = 2 * LANES
    loads[3].wait()
    loads[4].wait()
    for c in range(0, LN, step):
        corr = jnp.dot(cross_ref[...], lag_ref[:, c : c + step], preferred_element_type=f32)
        inv = jnp.dot(
            chosen, parts_ref[:, 2 * BAND + c : 2 * BAND + c + step], preferred_element_type=f32
        )
        normed = corr * (inv + unsent) * scale_ref[...]
        for k in range(step // LANES):
            line_ref[pl.ds(c // LANES + k, wide, stride=LN // LANES), :] = normed[
                :, LANES * k : LANES * (k + 1)
            ]

    loads[5].wait()
    loads[6].wait()
    rows_out = OUT // LANES
    lane4 = lax.broadcasted_iota(jnp.int32, (rows_out, LANES), 1)

    def one_template(t, carry):
        total_score = jnp.zeros((rows_out, LANES), f32)
        used = active_ref[0, t]
        for j in range(slots):
            move = move_ref[j, 0, t]
            q, s = move >> 7, move & (LANES - 1)
            start = (j * templs + t) * (LN // LANES) + q
            first = line_ref[pl.ds(start, rows_out), :]
            second = line_ref[pl.ds(start + 1, rows_out), :]
            joined = jnp.where(lane4 >= s, first, second)
            turned = pltpu.roll(joined, (LANES - s) & (LANES - 1), 1)
            total_score += turned * jnp.where(j < used, 1.0, 0.0)
        sums_ref[pl.ds(t * rows_out, rows_out), :] = total_score
        return carry

    lax.fori_loop(0, templs, one_template, 0, unroll=8)
    for a in range(rows_out):
        out_ref[:, LANES * a : LANES * (a + 1)] = sums_ref[pl.ds(a, templs, stride=rows_out), :]


def on_device(
    geometry, waveforms, templates, channel_ids, moveouts, active, border, border_count
):
    regions, tmpls, subs, offsets = geometry
    devices = tmpls * subs * len(offsets)
    chans = waveforms.shape[1]
    bmax = border.shape[2]
    templs, slots = channel_ids.shape[1:]
    wide = slots * templs
    by_slot = lambda x: jnp.transpose(x, (2, 0, 1))
    short_table, lag_table = wide_tables()
    pay_rows = -(-(chans * CHUNKS + 3) // 8) * 8
    vmem = pl.BlockSpec(memory_space=pltpu.VMEM)
    hbm = pl.BlockSpec(memory_space=pltpu.HBM)
    f32, bf16 = jnp.float32, jnp.bfloat16
    gather, spread, twiddle, fwd, inv, window = small_tables(chans)
    rows = jnp.swapaxes(templates[0], 0, 1).reshape(wide, K)
    inputs = (
        waveforms[0], gather, twiddle, fwd, inv, spread, window, border[0], border_count, rows,
        short_table,
    )
    recv, tspec, scale = pl.pallas_call(
        functools.partial(station_kernel, geometry),
        out_shape=(
            jax.ShapeDtypeStruct((devices, pay_rows, LANES), f32),
            jax.ShapeDtypeStruct((wide, 2 * BAND), f32),
            jax.ShapeDtypeStruct((wide, 1), f32),
        ),
        in_specs=[hbm] * STATION_INPUTS,
        out_specs=(hbm, hbm, hbm),
        scratch_shapes=[
            pltpu.VMEM((pay_rows, LANES), f32),
            pltpu.VMEM((RES * chans, LANES), f32),
            pltpu.VMEM((chans, 2 * BAND), f32),
            *[pltpu.VMEM(x.shape, x.dtype) for x in inputs],
            pltpu.VMEM((wide, 2 * BAND), f32),
            pltpu.VMEM((wide, 1), f32),
            pltpu.SemaphoreType.DMA((STATION_INPUTS,)),
            pltpu.SemaphoreType.DMA((devices,)),
            pltpu.SemaphoreType.DMA((devices,)),
        ],
        compiler_params=pltpu.CompilerParams(collective_id=0, has_side_effects=True),
        name="stations",
    )(*inputs)
    inputs = (recv, by_slot(channel_ids), tspec, lag_table, scale, by_slot(moveouts), active)
    spaces = [pltpu.VMEM] * 5 + [pltpu.SMEM] * 2
    scores = pl.pallas_call(
        functools.partial(match_kernel, geometry, chans, bmax),
        out_shape=jax.ShapeDtypeStruct((templs, OUT), f32),
        in_specs=[hbm] * MATCH_INPUTS,
        out_specs=vmem,
        scratch_shapes=[
            *[space(x.shape, x.dtype) for space, x in zip(spaces, inputs)],
            pltpu.VMEM((chans * devices, CHUNKS * LANES), f32),
            pltpu.VMEM((3 * chans * devices, CHUNKS * LANES), bf16),
            pltpu.VMEM((wide, 2 * BAND), bf16),
            pltpu.VMEM((wide * (LN // LANES), LANES), f32),
            pltpu.VMEM((templs * (OUT // LANES), LANES), f32),
            pltpu.SemaphoreType.DMA((MATCH_INPUTS,)),
        ],
        name="match",
    )(*inputs)
    return scores[None]


def solution(mesh):
    regions, tmpls, subs = (mesh.shape[a] for a in ("region", "tmpl", "sub"))
    offsets = tuple(dict.fromkeys((0, (regions - 1) % regions, 1 % regions)))
    geometry = (regions, tmpls, subs, offsets)
    in_specs = (
        P("region", ("tmpl", "sub"), "groups"),
        P("region", ("tmpl", "sub"), None, None),
        P("region", ("tmpl", "sub"), None),
        P("region", ("tmpl", "sub"), None),
        P("region", ("tmpl", "sub")),
        P("region", None, None),
        P("region", None),
    )
    return jax.shard_map(
        functools.partial(on_device, geometry),
        mesh=mesh,
        in_specs=in_specs,
        out_specs=P("region", ("tmpl", "sub"), "groups"),
        check_vma=False,
    )
```
